1024 devices in a mesh: group: 8 (over y_lo, x), member: 128 (over z, y_hi, core).
Axes of the slice: x: 4, y: 8 (y_hi: 4, y_lo: 2; y = y_hi * 2 + y_lo), z: 16, core: 2. Of those that a mesh axis runs over, the one named last changes fastest.
Arguments:
- points: bfloat16 [262144, 768], P(('group', 'member')), may hold values from -9 to 9
- centroids: bfloat16 [16384, 768], P('group'), may hold values from -5 to 5
- dest_group: int32 [262144, 1], P(('group', 'member')), may hold values from 0 to 7; in each aligned block of 256 rows (0 to 255, 256 to 511, ...) at most 64 rows name the same one
Outputs:
- refined: bfloat16 [16384, 768], P(('group', 'member'))
The draws below stay inside these ranges and needn't reach their ends.
Inputs may be any that keep to these rules, and one draw needn't show every extreme that they name: `dest_group`: among the 256 rows of one device, at most 64 name the same group, a bound that some block reaches of them.
All inputs are finite; a program needn't handle non-finite values.
Results may differ from the reference program's by a relative error of at most 0.0025.
Values may be sent and summed in bfloat16 or wider, within the bound.
A program may use at most 64 MiB of HBM per device.

```python
import math
import jax
import jax.numpy as jnp
import numpy as np
from jax import lax

D = 768
FINE = 2048
PTS_DEV = 256
CAP = 64
POINTS = 262144
CENTS = 16384
N_GROUP = 8
N_MEMBER = 128


def draw_centroids(key, part):
    values = jnp.clip(jax.random.normal(jax.random.fold_in(key, 11), (CENTS, D), jnp.float32), -5.0, 5.0)
    return values.astype(jnp.bfloat16)


def draw_points(key, part):
    values = jnp.clip(jax.random.normal(jax.random.fold_in(key, 12), (POINTS, D), jnp.float32), -5.0, 5.0)
    return values.astype(jnp.bfloat16)


def routed_block(rng, own, number, rows, amount, top, bound, skew):
    ranking = jax.random.permutation(rng, amount)
    crowded, common = shares(amount, rows * top, bound, skew, True), shares(amount, rows * top, bound, skew, False)
    places = jnp.arange(amount)

    def named(sizes, turn):
        used = int((sizes > 0).sum())
        fixed = max(1, used // 4)
        shifted = fixed + (places - fixed + turn * (used - fixed)) % max(1, amount - fixed)
        return jnp.zeros((amount,), jnp.int32).at[ranking[jnp.where(places < fixed, places, shifted)]].set(jnp.asarray(sizes, jnp.int32))

    sizes = jnp.where(number % 4 == 0, named(crowded, number // 4), named(common, number - number // 4 - 1))
    mixed = jax.random.permutation(jax.random.fold_in(own, 3), amount)
    giver, taker = mixed[0:amount // 2 * 2:2], mixed[1:amount // 2 * 2:2]
    slack = jnp.minimum(sizes[giver] - 1, bound - sizes[taker]) // 2
    slack = jnp.where((giver == ranking[0]) | (taker == ranking[0]) | (sizes[taker] == 0), 0, jnp.maximum(slack, 0))
    shifted = jax.random.randint(jax.random.fold_in(own, 4), (amount // 2,), 0, 1 << 20) % (slack + 1)
    sizes = sizes.at[giver].add(-shifted).at[taker].add(shifted)
    items = jnp.searchsorted(jnp.cumsum(sizes), jnp.arange(rows * top), side="right").astype(jnp.int32)
    listing = items.reshape(top, rows).T
    listing = listing[jax.random.permutation(jax.random.fold_in(own, 1), rows)]
    turn = jax.random.randint(jax.random.fold_in(own, 2), (rows, 1), 0, top)
    return jnp.take_along_axis(listing, (jnp.arange(top)[None, :] + turn) % top, axis=1)


def shares(count, total, reach, lean, full):
    portions = [(1 << 20) // math.isqrt(standing ** lean) + 1 for standing in range(1, count + 1)]
    largest = reach if full else min(reach, max(-(-total // count), total * portions[0] // sum(portions)))
    least = 1 if total - largest >= count - 1 else 0
    given, rest = [largest] + [least] * (count - 1), total - largest - least * (count - 1)
    while rest > 0:
        free = [i for i in range(1, count) if given[i] < largest] or [i for i in range(1, count) if given[i] < reach]
        whole, left = sum([portions[i] for i in free]), rest
        for i in free:
            addition = min(reach - given[i], max(1, left * portions[i] // whole), rest)
            given[i] = given[i] + addition
            rest = rest - addition
    return np.array(given)


def setup_inputs(seed: int = 0) -> dict:
    splits = jax.random.split(jax.random.key(seed), 4)
    points = draw_points(jax.random.fold_in(splits[3], 71), 0)
    centroids = draw_centroids(jax.random.fold_in(splits[3], 71), 0)
    dest_group_keys = jax.random.split(jax.random.fold_in(splits[2], 1), POINTS // PTS_DEV)
    dest_group_turns = jax.random.permutation(jax.random.fold_in(splits[2], 3), POINTS // PTS_DEV)
    dest_group = jax.vmap(lambda own, number: routed_block(jax.random.fold_in(splits[2], 2), own, number, PTS_DEV, N_GROUP, 1, CAP, 2))(dest_group_keys, dest_group_turns).reshape((POINTS, 1))
    return {"points": points, "centroids": centroids, "dest_group": dest_group}


score_scale = 0.15


def reference(points, centroids, dest_group):
    destination = dest_group[:, 0].astype(jnp.int32)
    order = jnp.argsort(destination, stable=True).astype(jnp.int32)
    sorted_points = points[order]
    group_rows = N_GROUP * N_MEMBER * CAP
    block_rows = N_GROUP * CAP
    padded = jnp.concatenate([sorted_points, jnp.zeros((group_rows, D), points.dtype)], axis=0)
    per_group = jnp.sum((destination[None, :] == jnp.arange(N_GROUP, dtype=jnp.int32)[:, None]).astype(jnp.int32), axis=1).astype(jnp.int32)
    starts = (jnp.cumsum(per_group) - per_group).astype(jnp.int32)

    def refit(group_index):
        table = lax.dynamic_slice_in_dim(centroids, (group_index * FINE).astype(jnp.int32), FINE, 0)
        table_f = table.astype(jnp.float32)
        norms = jnp.sum(table_f * table_f, axis=1)
        start = starts[group_index]
        count = per_group[group_index]

        def step(carry, block_index):
            sums, counts = carry
            offset = (block_index * block_rows).astype(jnp.int32)
            rows = lax.dynamic_slice_in_dim(padded, (start + offset).astype(jnp.int32), block_rows, 0)
            valid = ((offset + jnp.arange(block_rows, dtype=jnp.int32)) < count).astype(jnp.float32)
            scores = score_scale * (jnp.dot(rows, table.T, preferred_element_type=jnp.float32) - 0.5 * norms[None, :])
            weights = (jax.nn.softmax(scores, axis=-1) * valid[:, None]).astype(jnp.bfloat16)
            sums = sums + jnp.dot(weights.T, rows, preferred_element_type=jnp.float32)
            counts = counts + jnp.sum(weights.astype(jnp.float32), axis=0)
            return (sums, counts), None

        init = (jnp.zeros((FINE, D), jnp.float32), jnp.zeros((FINE,), jnp.float32))
        (sums, counts), _ = lax.scan(step, init, jnp.arange(group_rows // block_rows, dtype=jnp.int32))
        return ((sums + table_f) / (counts + 1.0)[:, None]).astype(jnp.bfloat16)

    result = lax.map(refit, jnp.arange(N_GROUP, dtype=jnp.int32))
    return result.reshape(CENTS, D)
```

```python
import functools

import jax
import jax.numpy as jnp
from jax import lax
from jax.experimental import pallas as pl
from jax.experimental.pallas import tpu as pltpu
from jax.sharding import PartitionSpec as P

MESH = pl.DeviceIdType.MESH
SCALE = 0.15
UNUSED = 64.0
CORES = 2
HIGH_Y = 4
F32, BF16, I32 = jnp.float32, jnp.bfloat16, jnp.int32
NT = (((1,), (1,)), ((), ()))


def iota(shape, dim):
    return lax.broadcasted_iota(I32, shape, dim)


def refit(
    groups, depth, wide, batch,
    points, table, dest, out,
    rows_in, packed, rows, cents, half_norms, scores, weights, sums, counts,
    stats, other_stats, z_out, z_in, zc_out, zc_in, total, y_out, y_in, yc_out, yc_in,
    load_sem, table_sem, a_send, a_recv, f_send, f_recv, s_send, s_recv,
    z_send, z_recv, zc_send, zc_recv, y_send, y_recv, yc_send, yc_recv,
):
    count, width = points.shape
    capacity = packed.shape[1]
    piece = cents.shape[2]
    chunk = wide * piece
    half_depth = depth // 2
    along_x = groups // 2
    block = along_x * capacity

    g, me = lax.axis_index("group"), lax.axis_index("member")
    core = lax.rem(me, CORES)
    y = lax.rem(lax.div(me, CORES), wide)
    z = lax.div(me, CORES * wide)
    gx, gy = lax.rem(g, along_x), lax.div(g, along_x)

    def member(zz, yy, cc):
        return (zz * wide + yy) * CORES + cc

    partner = (g, member(z, y, 1 - core))
    group_peers = {}
    for r in range(1, groups):
        dy, dx = r // along_x, r % along_x
        group_peers[r] = lax.rem(gy + dy, 2) * along_x + lax.rem(gx + dx, along_x)
    up = (g, member(lax.rem(z + 1, depth), y, core))
    down = (g, member(lax.rem(z + depth - 1, depth), y, core))
    y_peers = [lax.rem(y + r, wide) for r in range(1, wide)]

    def z_chunk(j):
        away = half_depth - j // 2 if j % 2 == 0 else half_depth + (j + 1) // 2
        return lax.rem(z + away, depth)

    load = pltpu.make_async_copy(points, rows_in, load_sem)
    load.start()
    table_loads = []
    for j in range(depth):
        table_loads.append(
            pltpu.make_async_copy(table.at[z_chunk(j), :, core], cents.at[j], table_sem.at[j])
        )
        table_loads[-1].start()

    barrier = pltpu.get_barrier_semaphore()
    greeted = [(group_peers[r], me) for r in range(1, groups)]
    greeted += [partner, up, down] + [(g, member(z, yy, core)) for yy in y_peers]
    for peer in greeted:
        pl.semaphore_signal(barrier, inc=1, device_id=peer, device_id_type=MESH)

    destination = dest[...]
    named = iota((16, count), 0) == destination
    earlier = (iota((count, count), 0) < iota((count, count), 1)).astype(F32).astype(BF16)
    before = jnp.dot(named.astype(F32).astype(BF16), earlier, preferred_element_type=F32)
    rank = jnp.sum(jnp.where(named, before, 0.0), axis=0, keepdims=True)
    slot = destination * capacity + rank.astype(I32)
    slots = groups * capacity
    place = (iota((slots, count), 0) == slot).astype(F32).astype(BF16)
    load.wait()
    moved = jnp.dot(place, rows_in[...], preferred_element_type=F32)
    used = jnp.dot(place, jnp.ones((count, 128), BF16), preferred_element_type=F32)
    mark = jnp.where((iota((slots, 128), 1) == 0) & (used < 0.5), UNUSED, 0.0)
    packed[:, :, :128] = (moved[:, :128] + mark).astype(BF16).reshape(groups, capacity, 128)
    packed[:, :, 128:] = moved[:, 128:].astype(BF16).reshape(groups, capacity, width - 128)

    pl.semaphore_wait(barrier, len(greeted))

    started = []

    def send(src, dst, send_sem, recv_sem, to):
        copy = pltpu.make_async_remote_copy(
            src_ref=src, dst_ref=dst, send_sem=send_sem, recv_sem=recv_sem,
            device_id=to, device_id_type=MESH,
        )
        copy.start()
        started.append(copy)
        return copy

    arrivals = {}
    for r in range(1, groups):
        arrivals[r] = send(
            packed.at[group_peers[r]], rows.at[0, r], a_send.at[r], a_recv.at[r],
            (group_peers[r], me),
        )
    forwards = [send(packed.at[g], rows.at[1, 0], f_send.at[0], f_recv.at[0], partner)]
    rows[0, 0] = packed[g]

    def forward(r):
        arrivals[r].wait_recv()
        forwards.append(
            send(rows.at[0, r], rows.at[1, r], f_send.at[r], f_recv.at[r], partner)
        )

    for j in range(depth):
        table_loads[j].wait()
    per = batch * chunk

    @pl.loop(0, depth // batch)
    def _(i):
        c = cents[pl.ds(i * batch, batch)].reshape(per, width).astype(F32)
        half_norms[pl.ds(i * per, per)] = 0.5 * jnp.sum(c * c, axis=1, keepdims=True)

    first = ((iota((16, width), 0) == 0) & (iota((16, width), 1) == 0)).astype(F32).astype(BF16)

    def score(b):
        half, quarter = divmod(b, 2)
        x = rows[half, quarter * along_x : (quarter + 1) * along_x].reshape(block, width)

        def raw(i, top):
            at = pl.ds(i * per, per)
            c = cents[pl.ds(i * batch, batch)].reshape(per, width)
            s = lax.dot_general(c, x, NT, preferred_element_type=F32)
            s = SCALE * (s - half_norms[at])
            scores[b, at] = s
            return jnp.maximum(top, jnp.max(s.reshape(per // 8, 8, block), axis=0))

        top = lax.fori_loop(0, depth // batch, raw, jnp.full((8, block), -jnp.inf, F32))
        top = jnp.max(top, axis=0, keepdims=True)

        def exps(i, low):
            at = pl.ds(i * per, per)
            e = jnp.exp(scores[b, at] - top)
            scores[b, at] = e
            return low + jnp.sum(e.reshape(per // 8, 8, block), axis=0)

        low = lax.fori_loop(0, depth // batch, exps, jnp.zeros((8, block), F32))
        low = jnp.sum(low, axis=0, keepdims=True)
        stats[b, 0] = jnp.broadcast_to(top, (8, block))
        stats[b, 1] = jnp.broadcast_to(low, (8, block))
        send(stats.at[b], other_stats.at[(b + 2) % 4], s_send.at[b], s_recv.at[(b + 2) % 4], partner)
        column = lax.dot_general(first, x, NT, preferred_element_type=F32)
        return top, low, column[:1] < 0.5 * UNUSED

    for r in range(1, along_x):
        forward(r)
    blocks = [score(0)]
    for r in range(along_x, groups):
        forward(r)
    blocks.append(score(1))
    for r in range(along_x):
        forwards[r].wait_recv()
    blocks.append(score(2))
    for r in range(along_x, groups):
        forwards[r].wait_recv()
    blocks.append(score(3))

    def share(b):
        top, low, valid = blocks[b]
        pltpu.make_async_remote_copy(
            src_ref=stats.at[b], dst_ref=other_stats.at[b], send_sem=s_send.at[b],
            recv_sem=s_recv.at[b], device_id=partner, device_id_type=MESH,
        ).wait_recv()
        their_top, their_low = other_stats[b, 0][:1], other_stats[b, 1][:1]
        highest = jnp.maximum(top, their_top)
        mine = jnp.exp(top - highest)
        whole = low * mine + their_low * jnp.exp(their_top - highest)
        return jnp.where(valid, mine / whole, 0.0)

    shares = [share(b) for b in range(4)]
    diagonal = iota((chunk, 128), 0) == iota((chunk, 128), 1)

    def weigh(i):
        at = slice(i * per, (i + 1) * per)
        seen = jnp.zeros((per, 128), F32)
        for b in range(4):
            w = (scores[b, at] * shares[b]).astype(BF16)
            weights[at, b * block : (b + 1) * block] = w
            wide_w = w.astype(F32)
            for k in range(0, block, 128):
                seen = seen + wide_w[:, k : k + 128]
        column = jnp.sum(seen, axis=1, keepdims=True)
        for k in range(batch):
            part = column[k * chunk : (k + 1) * chunk]
            line = jnp.sum(jnp.where(diagonal, part, 0.0), axis=0, keepdims=True)
            counts[i * batch + k] = jnp.broadcast_to(line, (8, 128))
        sums[at] = jnp.dot(
            weights[at], rows[...].reshape(2 * groups * capacity, width), preferred_element_type=F32
        )

    half = chunk // 2

    def from_ring(d, t, u):
        z_copies[d, t, u].wait_recv()
        return z_in[d, t, u].astype(F32)

    def count_from_ring(d, t):
        zc_copies[d, t].wait_recv()
        return zc_in[d, t]

    z_copies, zc_copies = {}, {}

    def ring(t):
        ways = [(0, up)] + ([(1, down)] if t < half_depth - 1 else [])
        for u in range(2):
            for d, to in ways:
                j = 2 * t + d
                v = sums[j * chunk + u * half : j * chunk + (u + 1) * half]
                if t > 0:
                    v = v + from_ring(d, t - 1, u)
                z_out[d, t, u] = v.astype(BF16)
                z_copies[d, t, u] = send(
                    z_out.at[d, t, u], z_in.at[d, t, u], z_send.at[d, t, u], z_recv.at[d, t, u], to
                )
        for d, to in ways:
            v = counts[2 * t + d]
            if t > 0:
                v = v + count_from_ring(d, t - 1)
            zc_out[d, t] = v
            zc_copies[d, t] = send(
                zc_out.at[d, t], zc_in.at[d, t], zc_send.at[d, t], zc_recv.at[d, t], to
            )

    weigh(0)
    made = 1
    for t in range(half_depth):
        while made <= (2 * t + 1) // batch:
            weigh(made)
            made += 1
        ring(t)
        if made < depth // batch:
            weigh(made)
            made += 1
    while made < depth // batch:
        weigh(made)
        made += 1

    own = (depth - 1) * chunk
    for u in range(2):
        v = sums[own + u * half : own + (u + 1) * half]
        v = v + from_ring(0, half_depth - 1, u)
        if half_depth > 1:
            v = v + from_ring(1, half_depth - 2, u)
        pieces = half // piece
        total[u * pieces : (u + 1) * pieces] = v.reshape(pieces, piece, width)
        y_out[u * pieces : (u + 1) * pieces] = v.astype(BF16).reshape(pieces, piece, width)
    seen = counts[depth - 1] + count_from_ring(0, half_depth - 1)
    if half_depth > 1:
        seen = seen + count_from_ring(1, half_depth - 2)
    yc_out[...] = seen

    y_copies = []
    for k, yy in enumerate(y_peers):
        to = (g, member(z, yy, core))
        y_copies.append(
            (
                send(y_out.at[yy], y_in.at[k], y_send.at[k], y_recv.at[k], to),
                send(yc_out, yc_in.at[k], yc_send.at[k], yc_recv.at[k], to),
            )
        )
    new = total[y]
    for k, (copy, count_copy) in enumerate(y_copies):
        copy.wait_recv()
        new = new + y_in[k].astype(F32)
        count_copy.wait_recv()
        seen = seen + yc_in[k]
    pick = iota((piece, 128), 1) == iota((piece, 128), 0) + y * piece
    soft_count = jnp.sum(
        jnp.where(pick, jnp.broadcast_to(seen[:1], (piece, 128)), 0.0), axis=1, keepdims=True
    )
    old = cents[depth - 1, y].astype(F32)
    out[...] = ((new + old) / (soft_count + 1.0)).astype(BF16)

    for copy in started:
        copy.wait_send()


def build(mesh, wide, batch):
    groups, members = mesh.shape["group"], mesh.shape["member"]
    depth = members // (CORES * wide)

    def local(points, centroids, dest_group):
        count, width = points.shape
        fine = centroids.shape[0]
        piece = fine // members
        capacity = count // 4 if groups >= 4 else count // groups
        chunk = wide * piece
        half_fine = depth * chunk
        block = groups // 2 * capacity
        steps = depth // 2
        dma = pltpu.SemaphoreType.DMA
        vmem = pltpu.VMEM
        scratch = [
            vmem((count, width), BF16),
            vmem((groups, capacity, width), BF16),
            vmem((2, groups, capacity, width), BF16),
            vmem((depth, wide, piece, width), BF16),
            vmem((half_fine, 1), F32),
            vmem((4, half_fine, block), F32),
            vmem((half_fine, 4 * block), BF16),
            vmem((half_fine, width), F32),
            vmem((depth, 8, 128), F32),
            vmem((4, 2, 8, block), F32),
            vmem((4, 2, 8, block), F32),
            vmem((2, steps, 2, chunk // 2, width), BF16),
            vmem((2, steps, 2, chunk // 2, width), BF16),
            vmem((2, steps, 8, 128), F32),
            vmem((2, steps, 8, 128), F32),
            vmem((wide, piece, width), F32),
            vmem((wide, piece, width), BF16),
            vmem((wide - 1, piece, width), BF16),
            vmem((8, 128), F32),
            vmem((wide - 1, 8, 128), F32),
            dma,
            dma((depth,)),
            dma((groups,)), dma((groups,)), dma((groups,)), dma((groups,)),
            dma((4,)), dma((4,)),
            dma((2, steps, 2)), dma((2, steps, 2)), dma((2, steps)), dma((2, steps)),
            dma((wide - 1,)), dma((wide - 1,)), dma((wide - 1,)), dma((wide - 1,)),
        ]
        table = centroids.reshape(depth, wide, CORES, piece, width)
        return pl.pallas_call(
            functools.partial(refit, groups, depth, wide, batch),
            out_shape=jax.ShapeDtypeStruct((piece, width), BF16),
            in_specs=[
                pl.BlockSpec(memory_space=pl.ANY),
                pl.BlockSpec(memory_space=pl.ANY),
                pl.BlockSpec(memory_space=pltpu.VMEM),
            ],
            out_specs=pl.BlockSpec(memory_space=pltpu.VMEM),
            scratch_shapes=scratch,
            compiler_params=pltpu.CompilerParams(collective_id=0, has_side_effects=True),
            name="refit",
        )(points, table, dest_group.reshape(1, count))

    both = P(("group", "member"), None)
    return jax.shard_map(
        local, mesh=mesh, in_specs=(both, P("group", None), both), out_specs=both, check_vma=False
    )


def solution(mesh):
    return build(mesh, HIGH_Y, 4)
```
